32 devices in a mesh: leaf: 4 (over x, core), row: 4 (over z), col: 2 (over y).
Axes of the slice: x: 2, y: 2, z: 4, core: 2. Of those that a mesh axis runs over, the one named last changes fastest.
Arguments:
- widths: int32 [15], replicated, may hold values from 1024 to 2048, as said below
- bottom_lists: int32 [8, 32], P('leaf'), may hold values from 0 to 47, as said below
- root_inverse: bfloat16 [2048, 2048], P('row')
- second_panels: bfloat16 [4, 2048, 1024], P('leaf', 'row', 'col'), may hold values from -0.09375 to 0.09375
- second_inverse: bfloat16 [4, 1024, 2048], P('leaf', 'col', 'row')
- third_panels: bfloat16 [4, 2, 2048, 2048], P('leaf', None, 'row', 'col'), may hold values from -0.09375 to 0.09375
- third_inverse: bfloat16 [4, 2048, 2048], P('leaf', 'col', 'row')
- bottom_panels: bfloat16 [8, 4096, 2048], P('leaf', 'row', 'col'), may hold values from -0.09375 to 0.09375
- bottom_inverse: bfloat16 [8, 2048, 2048], P('leaf', 'col', 'row')
Outputs:
- second_off: bfloat16 [4, 2048, 1024], P('leaf', 'row', 'col')
- second_diag: bfloat16 [4, 1024, 2048], P('leaf', 'col', 'row')
- third_off: bfloat16 [4, 2, 2048, 2048], P('leaf', None, 'row', 'col')
- third_diag: bfloat16 [4, 2048, 2048], P('leaf', 'col', 'row')
- bottom_off: bfloat16 [8, 3, 2048, 2048], P('leaf', None, 'row', 'col')
- bottom_diag: bfloat16 [8, 2048, 2048], P('leaf', 'col', 'row')
The draws below stay inside these ranges and needn't reach their ends.
Inputs may be any that keep to these rules, and one draw needn't show every extreme that they name: `widths`: some supernode has 2048 columns and some 2048/2. `bottom_lists`: row e lists 32 different blocks of 128 rows of its chain (root, then second-level ancestor, then parent, 16 blocks each) in increasing order; block 0 and all blocks of the parent are always listed.
All inputs are finite; a program needn't handle non-finite values.
Results may differ from the reference program's by a relative error of at most 0.015.
Values may be sent and summed in bfloat16 or wider, within the bound.
No kernel may reach another device: no remote copies, remote signals or barrier semaphores. Data moves between devices by JAX's collectives and lax.ppermute only.
A program may use at most 192 MiB of HBM per device.

```python
import jax
import jax.numpy as jnp
from jax import lax

B = 2048
R = 128
NODES = 15
BOTTOM = 8
N_ROW = 4


def symmetric_blocks(key, count):
    base = jax.random.normal(key, (count, B, B), jnp.float32)
    return 0.35 * (base + jnp.swapaxes(base, 1, 2))


def draw_widths(key, part):
    picks = jax.random.randint(jax.random.fold_in(key, 1), (NODES,), B // 2, B + 1)
    order = jax.random.permutation(jax.random.fold_in(key, 2), NODES)
    picks = picks.at[order[0]].set(B).at[order[1]].set(B // 2)
    return picks.astype(jnp.int32)


def draw_bottom_lists(key, part):
    blocks = B // R

    def one_list(sub_key):
        upper_part = jax.random.permutation(sub_key, 2 * blocks - 1)[:blocks - 1] + 1
        chosen = jnp.concatenate([jnp.zeros((1,), jnp.int32), upper_part.astype(jnp.int32), jnp.arange(2 * blocks, 3 * blocks, dtype=jnp.int32)])
        return jnp.sort(chosen)
    return jax.vmap(one_list)(jax.random.split(jax.random.fold_in(key, 3), BOTTOM)).astype(jnp.int32)


def draw_root_inverse(key, part):
    return symmetric_blocks(jax.random.fold_in(key, 4), 1)[0].astype(jnp.bfloat16)


def draw_second_inverse(key, part):
    return symmetric_blocks(jax.random.fold_in(key, 5), 2).reshape(4, B // 2, B).astype(jnp.bfloat16)


def draw_third_inverse(key, part):
    return symmetric_blocks(jax.random.fold_in(key, 6), 4).astype(jnp.bfloat16)


def draw_bottom_inverse(key, part):
    return symmetric_blocks(jax.random.fold_in(key, 7), BOTTOM).astype(jnp.bfloat16)


def steps_of(stream_key, extent, shards, low, high):
    def one(axis_at, blocks):
        draws = jax.random.uniform(jax.random.fold_in(jax.random.fold_in(stream_key, 6), axis_at), (blocks,), jnp.float32, low / len(shards), high / len(shards))
        return jnp.repeat(jnp.exp(draws), extent[axis_at] // blocks).reshape((-1,) + (1,) * (len(extent) - axis_at - 1))

    factor_of = one(*shards[0])
    for cut in shards[1:]:
        factor_of = factor_of * one(*cut)
    return factor_of


def noise(own_key, dims, width, limit, cuts=(), kind=jnp.bfloat16):
    result = jax.random.normal(own_key, dims, jnp.float32) * width
    if len(cuts) > 0:
        result = steps_of(own_key, dims, cuts, -0.22, 0.18) * result
    return jnp.clip(result, min=-limit, max=limit).astype(kind)


def setup_inputs(seed: int = 0) -> dict:
    key_list = jax.random.split(jax.random.key(seed), 10)
    widths = draw_widths(jax.random.fold_in(key_list[9], 71), 0)
    bottom_lists = draw_bottom_lists(jax.random.fold_in(key_list[9], 71), 0)
    root_inverse = draw_root_inverse(jax.random.fold_in(key_list[9], 71), 0)
    second_panels = noise(key_list[3], (4, B, B // 2), (2 * B) ** -0.5, 0.09375, ((0, 4), (1, 4), (2, 2)))
    second_inverse = draw_second_inverse(jax.random.fold_in(key_list[9], 71), 0)
    third_panels = noise(key_list[5], (4, 2, B, B), (2 * B) ** -0.5, 0.09375, ((0, 4), (2, 4), (3, 2)))
    third_inverse = draw_third_inverse(jax.random.fold_in(key_list[9], 71), 0)
    bottom_panels = noise(key_list[7], (BOTTOM, 2 * B, B), (2 * B) ** -0.5, 0.09375, ((0, 4), (1, 4), (2, 2)))
    bottom_inverse = draw_bottom_inverse(jax.random.fold_in(key_list[9], 71), 0)
    return dict(widths=widths, bottom_lists=bottom_lists, root_inverse=root_inverse, second_panels=second_panels, second_inverse=second_inverse, third_panels=third_panels, third_inverse=third_inverse, bottom_panels=bottom_panels, bottom_inverse=bottom_inverse)


def node_mask(widths, node_at):
    return jnp.arange(B) < widths[node_at]


def both_mask(widths, node_at):
    ones_at = node_mask(widths, node_at)
    return ones_at[:, None] & ones_at[None, :]


def partial_sums(lower_rows, upper_rows):
    ancestors = lower_rows.shape[0]
    slab_rows = B // N_ROW
    lower_cut = jnp.transpose(lower_rows.reshape(ancestors, N_ROW, slab_rows, B), (1, 0, 2, 3))
    upper_cut = jnp.transpose(upper_rows.reshape(ancestors, N_ROW, slab_rows, B), (1, 0, 2, 3))

    def add_slab(running, pair_in):
        left_part, right_part = pair_in
        term_slab = jnp.einsum("kin,kim->nm", left_part.astype(jnp.float32), right_part.astype(jnp.float32))
        term_slab = lax.optimization_barrier(term_slab.astype(jnp.bfloat16))
        return running + term_slab.astype(jnp.float32), None

    running, _ = lax.scan(add_slab, jnp.zeros((B, B), jnp.float32), (lower_cut, upper_cut))
    return running


def reference(widths, bottom_lists, root_inverse, second_panels, second_inverse, third_panels, third_inverse, bottom_panels, bottom_inverse):
    root_block = jnp.where(both_mask(widths, 0), root_inverse, 0).astype(jnp.bfloat16)
    off_blocks = []
    diag_blocks = []
    off_halves = []
    diag_halves = []
    for parent in range(2):
        node_at = 1 + parent
        panel_at = jnp.concatenate([second_panels[2 * parent], second_panels[2 * parent + 1]], axis=1)
        panel_at = jnp.where(node_mask(widths, node_at)[None, :], panel_at, 0).astype(jnp.bfloat16)
        off_block = (-jnp.dot(root_block, panel_at, preferred_element_type=jnp.float32)).astype(jnp.bfloat16)
        inverse_at = jnp.concatenate([second_inverse[2 * parent], second_inverse[2 * parent + 1]], axis=0)
        masked_at = jnp.where(both_mask(widths, node_at), inverse_at.astype(jnp.float32), 0.0)
        diag_block = (masked_at - partial_sums(panel_at[None], off_block[None])).astype(jnp.bfloat16)
        off_blocks.append(off_block)
        diag_blocks.append(diag_block)
        off_halves += [off_block[:, : B // 2], off_block[:, B // 2:]]
        diag_halves += [diag_block[: B // 2], diag_block[B // 2:]]
    chains = []
    third_offs = []
    third_diags = []
    for group_at in range(4):
        parent = group_at // 2
        node_at = 3 + group_at
        chain_two = jnp.concatenate([
            jnp.concatenate([root_block, off_blocks[parent]], axis=1),
            jnp.concatenate([off_blocks[parent].T, diag_blocks[parent].T], axis=1)], axis=0)
        panel_at = third_panels[group_at].reshape(2 * B, B)
        panel_at = jnp.where(node_mask(widths, node_at)[None, :], panel_at, 0).astype(jnp.bfloat16)
        off_two = (-jnp.dot(chain_two, panel_at, preferred_element_type=jnp.float32)).astype(jnp.bfloat16)
        masked_at = jnp.where(both_mask(widths, node_at), third_inverse[group_at].astype(jnp.float32), 0.0)
        diag_two = (masked_at - partial_sums(panel_at.reshape(2, B, B), off_two.reshape(2, B, B))).astype(jnp.bfloat16)
        chain_three = jnp.concatenate([
            jnp.concatenate([chain_two, off_two], axis=1),
            jnp.concatenate([off_two.T, diag_two.T], axis=1)], axis=0)
        chains.append(chain_three)
        third_offs.append(off_two.reshape(2, B, B))
        third_diags.append(diag_two)
    spot_list = jnp.arange(2 * B, dtype=jnp.int32)
    bottom_offs = []
    bottom_diags = []
    for bottom in range(BOTTOM):
        node_at = NODES - BOTTOM + bottom
        chain_at = chains[bottom // 2]
        positions = (jnp.repeat(bottom_lists[bottom].astype(jnp.int32), R) * R + spot_list % R).astype(jnp.int32)
        panel_at = jnp.where(node_mask(widths, node_at)[None, :], bottom_panels[bottom], 0).astype(jnp.bfloat16)
        spread = jnp.zeros((3 * B, B), jnp.bfloat16).at[positions].set(panel_at)
        member = jnp.zeros((3 * B,), jnp.bool_).at[positions].set(True)
        product = jnp.dot(chain_at, spread, preferred_element_type=jnp.float32)
        off_three = jnp.where(member[:, None], -product, 0.0).astype(jnp.bfloat16)
        masked_at = jnp.where(both_mask(widths, node_at), bottom_inverse[bottom].astype(jnp.float32), 0.0)
        diag_three = (masked_at - partial_sums(spread.reshape(3, B, B), off_three.reshape(3, B, B))).astype(jnp.bfloat16)
        bottom_offs.append(off_three.reshape(3, B, B))
        bottom_diags.append(diag_three)
    return (jnp.stack(off_halves), jnp.stack(diag_halves), jnp.stack(third_offs), jnp.stack(third_diags),
            jnp.stack(bottom_offs), jnp.stack(bottom_diags))
```

```python
import jax
import jax.numpy as jnp
from jax import lax
from jax.experimental import pallas as pl
from jax.experimental.pallas import tpu as pltpu
from jax.sharding import PartitionSpec as P

NODES = 15
BOTTOM = 8


def partner(block, axis, apart):
    count = lax.axis_size(axis)
    route = []
    for low in range(count):
        high = low | 1 << apart
        if high != low and high < count:
            route += [(low, high), (high, low)]
    return lax.ppermute(block, axis, route)


def node_width(widths, node_at):
    return jnp.sum(jnp.where(jnp.arange(widths.shape[0]) == node_at, widths, 0))


def chain_fold(flat_chain, tile_width, ancestors, shard_piece):
    piece_rows = shard_piece.shape[1]
    picked = jnp.concatenate(
        [
            lax.dynamic_slice_in_dim(flat_chain, level_at * tile_width, piece_rows, 1)
            for level_at in range(ancestors)
        ],
        axis=1,
    )
    stacked = shard_piece.reshape(ancestors * piece_rows, shard_piece.shape[2])
    return jnp.dot(picked, stacked, preferred_element_type=jnp.float32)


def local_general(
    widths,
    bottom_lists,
    root_inverse,
    second_panels,
    second_inverse,
    third_panels,
    third_inverse,
    bottom_panels,
    bottom_inverse,
):
    group_at = lax.axis_index("leaf")
    row_at = lax.axis_index("row")
    col_at = lax.axis_index("col")
    rows_dev = root_inverse.shape[0]
    tile_width = root_inverse.shape[1]
    half_cols = second_panels.shape[2]
    own_cols = third_panels.shape[3]
    half_at = group_at % 2
    parent_one = 1 + group_at // 2
    node_two = 3 + group_at
    row_first = row_at * rows_dev
    row_index = row_first + jnp.arange(rows_dev)
    root_width = node_width(widths, 0)
    root_mask = (row_index < root_width)[:, None] & (jnp.arange(tile_width) < root_width)[None, :]
    root_block = jnp.where(root_mask, root_inverse, 0)
    width_one = node_width(widths, parent_one)
    mask_rows_one = row_index < width_one
    first_col = half_at * (tile_width // 2) + col_at * half_cols
    mask_cols_one = first_col + jnp.arange(half_cols) < width_one
    panel_one = jnp.where(mask_cols_one[None, :], second_panels[0], 0)
    shard_piece = lax.all_gather(panel_one, "row", axis=0, tiled=True)
    flat_piece = shard_piece
    product_one = jnp.dot(root_block, flat_piece, preferred_element_type=jnp.float32)
    off_one = (-product_one).astype(jnp.bfloat16)
    mine_half = lax.all_gather(off_one, "col", axis=1, tiled=True)
    other_half = partner(mine_half, "leaf", 0)
    off_full = jnp.where(
        half_at == 0,
        jnp.concatenate([mine_half, other_half], 1),
        jnp.concatenate([other_half, mine_half], 1),
    )
    term_one = lax.dot_general(
        panel_one, off_full, (((0,), (0,)), ((), ())), preferred_element_type=jnp.float32
    )
    summed_one = lax.psum_scatter(
        term_one.astype(jnp.bfloat16), "row", scatter_dimension=1, tiled=True
    ).astype(jnp.float32)
    inverse_one = jnp.where(
        mask_cols_one[:, None] & mask_rows_one[None, :], second_inverse[0], 0
    ).astype(jnp.float32)
    diag_one = (inverse_one - summed_one).astype(jnp.bfloat16)
    mine_diag = lax.all_gather(diag_one.T, "col", axis=1, tiled=True)
    other_diag = partner(mine_diag, "leaf", 0)
    diag_full = jnp.where(
        half_at == 0,
        jnp.concatenate([mine_diag, other_diag], 1),
        jnp.concatenate([other_diag, mine_diag], 1),
    )
    second_off = off_one[None]
    second_diag = diag_one[None]
    turned_one = lax.all_to_all(off_full, "row", split_axis=1, concat_axis=0, tiled=True)
    chain_two = jnp.stack(
        [jnp.concatenate([root_block, off_full], 1), jnp.concatenate([turned_one.T, diag_full], 1)],
        0,
    )
    flat_two = chain_two.reshape(2 * rows_dev, 2 * tile_width)
    first_own = col_at * own_cols
    width_two = node_width(widths, node_two)
    mask_cols_two = first_own + jnp.arange(own_cols) < width_two
    panel_two = jnp.where(mask_cols_two[None, None, :], third_panels[0], 0)
    product_two = chain_fold(
        flat_two, tile_width, 2, lax.all_gather(panel_two, "row", axis=1, tiled=True)
    )
    off_two = (-product_two).astype(jnp.bfloat16).reshape(2, rows_dev, own_cols)
    full_two = lax.all_gather(off_two, "col", axis=2, tiled=True)
    term_two = jnp.einsum("kin,kim->nm", panel_two, full_two, preferred_element_type=jnp.float32)
    summed_two = lax.psum_scatter(
        term_two.astype(jnp.bfloat16), "row", scatter_dimension=1, tiled=True
    ).astype(jnp.float32)
    mask_rows_two = row_index < width_two
    inverse_two = jnp.where(
        mask_cols_two[:, None] & mask_rows_two[None, :], third_inverse[0], 0
    ).astype(jnp.float32)
    diag_two = (inverse_two - summed_two).astype(jnp.bfloat16)
    diag_rows_two = lax.all_gather(diag_two.T, "col", axis=1, tiled=True)
    turned_two = lax.all_to_all(full_two, "row", split_axis=2, concat_axis=1, tiled=True)
    lower_two = jnp.transpose(turned_two, (2, 0, 1)).reshape(rows_dev, 2 * tile_width)
    chain_three = jnp.stack(
        [
            jnp.concatenate([chain_two[0], full_two[0]], 1),
            jnp.concatenate([chain_two[1], full_two[1]], 1),
            jnp.concatenate([lower_two, diag_rows_two], 1),
        ],
        0,
    )
    flat_three = chain_three.reshape(3 * rows_dev, 3 * tile_width)
    bottom_dev = bottom_panels.shape[0]
    list_len = bottom_lists.shape[1]
    block_rows = 2 * tile_width // list_len
    node_three = NODES - BOTTOM + bottom_dev * group_at + jnp.arange(bottom_dev)
    width_three = jnp.sum(
        jnp.where(jnp.arange(widths.shape[0])[None, :] == node_three[:, None], widths[None, :], 0),
        1,
    )
    mask_cols_three = (first_own + jnp.arange(own_cols))[None, :] < width_three[:, None]
    panel_three = jnp.where(mask_cols_three[:, None, :], bottom_panels, 0)
    positions = (
        jnp.repeat(bottom_lists, block_rows, axis=1) * block_rows
        + jnp.arange(list_len * block_rows) % block_rows
    )
    own_chain = (jnp.arange(3)[:, None] * tile_width + row_index[None, :]).reshape(-1)
    matches = bottom_lists[:, :, None] == (own_chain // block_rows)[None, None, :]
    member = jnp.any(matches, axis=1)
    slot_index = (
        jnp.sum(jnp.where(matches, jnp.arange(list_len)[None, :, None], 0), axis=1) * block_rows
        + own_chain % block_rows
    )
    shard_piece = lax.all_gather(panel_three, "row", axis=1, tiled=True)
    kept_rows = jnp.zeros((bottom_dev, 3 * rows_dev, own_cols), jnp.bfloat16)
    piece_rows = shard_piece.shape[1]
    columns = jnp.take(flat_three, positions.reshape(-1), axis=1).reshape(
        3 * rows_dev, bottom_dev, piece_rows
    )
    running = jnp.einsum("aec,ecn->ean", columns, shard_piece, preferred_element_type=jnp.float32)
    inside = member & (slot_index >= 0) & (slot_index < piece_rows)
    fetched = jax.vmap(lambda rows_in, picks: jnp.take(rows_in, picks, axis=0))(
        shard_piece, jnp.clip(slot_index, 0, piece_rows - 1)
    )
    kept_rows = jnp.where(inside[:, :, None], fetched, kept_rows)
    product_three, kept_rows = (running, kept_rows)
    chain_rows = kept_rows.reshape(bottom_dev, 3, rows_dev, own_cols)
    off_three = jnp.where(member[:, :, None], -product_three, 0.0).astype(jnp.bfloat16)
    off_three = off_three.reshape(bottom_dev, 3, rows_dev, own_cols)
    full_three = lax.all_gather(off_three, "col", axis=3, tiled=True)
    term_three = jnp.einsum(
        "ekin,ekim->enm", chain_rows, full_three, preferred_element_type=jnp.float32
    )
    summed_three = lax.psum_scatter(
        term_three.astype(jnp.bfloat16), "row", scatter_dimension=2, tiled=True
    ).astype(jnp.float32)
    mask_rows_three = row_index[None, :] < width_three[:, None]
    inverse_three = jnp.where(
        mask_cols_three[:, :, None] & mask_rows_three[:, None, :], bottom_inverse, 0
    ).astype(jnp.float32)
    diag_three = (inverse_three - summed_three).astype(jnp.bfloat16)
    return (second_off, second_diag, off_two[None], diag_two[None], off_three, diag_three)


def copy_block(picks, blocks_in, blocks_out):
    blocks_out[...] = blocks_in[...]


def pick_columns(matrix, picks, width):
    rows = matrix.shape[0]
    count = picks.shape[0]
    return pl.pallas_call(
        copy_block,
        out_shape=jax.ShapeDtypeStruct((rows, count * width), matrix.dtype),
        grid_spec=pltpu.PrefetchScalarGridSpec(
            num_scalar_prefetch=1,
            grid=(count,),
            in_specs=[pl.BlockSpec((rows, width), lambda j, picks: (0, picks[j]))],
            out_specs=pl.BlockSpec((rows, width), lambda j, picks: (0, j)),
        ),
        cost_estimate=pl.CostEstimate(
            flops=0, transcendentals=0, bytes_accessed=4 * rows * count * width
        ),
        name="pick_columns",
    )(picks, matrix)


def pick_rows(matrix, picks, height):
    columns = matrix.shape[1]
    count = picks.shape[0]
    return pl.pallas_call(
        copy_block,
        out_shape=jax.ShapeDtypeStruct((count * height, columns), matrix.dtype),
        grid_spec=pltpu.PrefetchScalarGridSpec(
            num_scalar_prefetch=1,
            grid=(count,),
            in_specs=[pl.BlockSpec((height, columns), lambda j, picks: (picks[j], 0))],
            out_specs=pl.BlockSpec((height, columns), lambda j, picks: (j, 0)),
        ),
        cost_estimate=pl.CostEstimate(
            flops=0, transcendentals=0, bytes_accessed=4 * columns * count * height
        ),
        name="pick_rows",
    )(picks, matrix)


def beside(mine, other, place, axis):
    return jnp.where(
        place == 0,
        jnp.concatenate([mine, other], axis),
        jnp.concatenate([other, mine], axis),
    )


def both_columns(block, col_at, axis):
    other = lax.ppermute(block, "col", [(0, 1), (1, 0)])
    return beside(block, other, col_at, axis)


def product(left, right):
    return jnp.dot(left, right, preferred_element_type=jnp.float32)


def inner(left, right):
    return lax.dot_general(
        left, right, (((0,), (0,)), ((), ())), preferred_element_type=jnp.float32
    )


def local_paired(
    widths,
    bottom_lists,
    root_inverse,
    second_panels,
    second_inverse,
    third_panels,
    third_inverse,
    bottom_panels,
    bottom_inverse,
):
    group_at = lax.axis_index("leaf")
    row_at = lax.axis_index("row")
    col_at = lax.axis_index("col")
    rows_dev = root_inverse.shape[0]
    tile_width = root_inverse.shape[1]
    half_cols = second_panels.shape[2]
    own_cols = third_panels.shape[3]
    half_at = group_at % 2
    row_first = row_at * rows_dev
    first_own = col_at * own_cols
    row_index = row_first + jnp.arange(rows_dev)
    all_index = jnp.arange(tile_width)
    own_index = first_own + jnp.arange(own_cols)

    root_width = node_width(widths, 0)
    root_mask = (row_index < root_width)[:, None] & (all_index < root_width)[None, :]
    root_block = jnp.where(root_mask, root_inverse, 0)
    shares = lax.axis_size("leaf") * lax.axis_size("col")
    share_rows = rows_dev // shares
    share_at = group_at * lax.axis_size("col") + col_at
    root_share = lax.dynamic_slice_in_dim(root_block, share_at * share_rows, share_rows, 0)
    root_full = lax.all_gather(root_share, ("row", "leaf", "col"), axis=0, tiled=True)

    panel_quarter = lax.all_gather(second_panels[0], "row", axis=0, tiled=True)
    panel_half = both_columns(panel_quarter, col_at, 1)
    panel_one = beside(panel_half, partner(panel_half, "leaf", 0), half_at, 1)
    inverse_half = both_columns(second_inverse[0], col_at, 0)
    inverse_one = beside(inverse_half, partner(inverse_half, "leaf", 0), half_at, 0)

    width_one = node_width(widths, 1 + group_at // 2)
    keep_one = all_index < width_one
    keep_rows_one = row_index < width_one
    off_one = jnp.where(keep_one[None, :], -product(root_block, panel_one), 0).astype(jnp.bfloat16)
    panel_turn = lax.dynamic_slice_in_dim(panel_one, row_first, rows_dev, 1)
    turn_one = jnp.where(keep_rows_one[None, :], -product(root_full, panel_turn), 0).astype(
        jnp.bfloat16
    )
    mask_one = keep_one[:, None] & keep_rows_one[None, :]
    diag_one = jnp.where(
        mask_one, inverse_one.astype(jnp.float32) - inner(panel_one, turn_one), 0
    ).astype(jnp.bfloat16)
    quarter_first = half_at * (tile_width // 2) + col_at * half_cols
    second_off = lax.dynamic_slice_in_dim(off_one, quarter_first, half_cols, 1)[None]
    second_diag = lax.dynamic_slice_in_dim(diag_one, quarter_first, half_cols, 0)[None]
    upper_two = jnp.concatenate([root_block, off_one], 1)
    lower_two = jnp.concatenate([turn_one, diag_one], 0).T
    chain_two = jnp.concatenate([upper_two, lower_two], 0)

    panel_two = lax.all_gather(third_panels[0], "row", axis=1, tiled=True)
    panel_two = panel_two.reshape(2 * tile_width, own_cols)
    width_two = node_width(widths, 3 + group_at)
    keep_two = own_index < width_two
    keep_rows_two = row_index < width_two
    off_two = jnp.where(keep_two[None, :], -product(chain_two, panel_two), 0).astype(jnp.bfloat16)
    off_two = off_two.reshape(2, rows_dev, own_cols)
    full_two = both_columns(off_two, col_at, 2)
    turn_share = lax.dynamic_index_in_dim(full_two, col_at, 0, keepdims=False)
    turn_share = lax.all_to_all(turn_share, "row", split_axis=1, concat_axis=0, tiled=True)
    turn_two = both_columns(turn_share, col_at, 0)
    mask_two = keep_two[:, None] & keep_rows_two[None, :]
    diag_two = jnp.where(
        mask_two, third_inverse[0].astype(jnp.float32) - inner(panel_two, turn_two), 0
    ).astype(jnp.bfloat16)
    diag_full = both_columns(diag_two, col_at, 0)
    chain_three = jnp.concatenate(
        [
            jnp.concatenate([chain_two, full_two.reshape(2 * rows_dev, tile_width)], 1),
            jnp.concatenate([turn_two, diag_full], 0).T,
        ],
        0,
    )

    bottom_dev = bottom_panels.shape[0]
    list_len = bottom_lists.shape[1]
    block_rows = 2 * tile_width // list_len
    dev_blocks = rows_dev // block_rows
    chain_blocks = (
        jnp.arange(3)[:, None] * (tile_width // block_rows)
        + row_at * dev_blocks
        + jnp.arange(dev_blocks)[None, :]
    ).reshape(-1)
    offs = []
    diags = []
    for at in range(bottom_dev):
        listed = bottom_lists[at]
        matches = listed[:, None] == chain_blocks[None, :]
        member = jnp.any(matches, axis=0)
        slots = jnp.sum(jnp.where(matches, jnp.arange(list_len)[:, None], 0), axis=0)
        member_rows = jnp.repeat(member, block_rows)
        width_three = node_width(widths, NODES - BOTTOM + bottom_dev * group_at + at)
        keep_three = own_index < width_three
        keep_rows_three = row_index < width_three
        panel_three = lax.all_gather(bottom_panels[at], "row", axis=0, tiled=True)
        chain_listed = pick_columns(chain_three, listed, block_rows)
        off_three = jnp.where(
            member_rows[:, None] & keep_three[None, :], -product(chain_listed, panel_three), 0
        ).astype(jnp.bfloat16)
        full_three = both_columns(off_three, col_at, 1)
        kept_rows = pick_rows(panel_three, slots, block_rows)
        term_three = inner(kept_rows, full_three).astype(jnp.bfloat16)
        summed_three = lax.psum_scatter(term_three, "row", scatter_dimension=1, tiled=True)
        mask_three = keep_three[:, None] & keep_rows_three[None, :]
        diags.append(
            jnp.where(
                mask_three,
                bottom_inverse[at].astype(jnp.float32) - summed_three.astype(jnp.float32),
                0,
            ).astype(jnp.bfloat16)
        )
        offs.append(off_three.reshape(3, rows_dev, own_cols))
    return (
        second_off,
        second_diag,
        off_two[None],
        diag_two[None],
        jnp.stack(offs),
        jnp.stack(diags),
    )


def solution(mesh):
    in_specs = (
        P(),
        P("leaf", None),
        P("row", None),
        P("leaf", "row", "col"),
        P("leaf", "col", "row"),
        P("leaf", None, "row", "col"),
        P("leaf", "col", "row"),
        P("leaf", "row", "col"),
        P("leaf", "col", "row"),
    )
    out_specs = (
        P("leaf", "row", "col"),
        P("leaf", "col", "row"),
        P("leaf", None, "row", "col"),
        P("leaf", "col", "row"),
        P("leaf", None, "row", "col"),
        P("leaf", "col", "row"),
    )
    body = local_paired if mesh.shape["col"] == 2 else local_general
    return jax.shard_map(body, mesh=mesh, in_specs=in_specs, out_specs=out_specs, check_vma=False)
```

```python
import jax
import jax.numpy as jnp
from jax import lax
from jax.experimental import pallas as pl
from jax.experimental.pallas import tpu as pltpu
from jax.sharding import PartitionSpec as P

NODES = 15
BOTTOM = 8


def partner(block, axis, apart):
    count = lax.axis_size(axis)
    route = []
    for low in range(count):
        high = low | 1 << apart
        if high != low and high < count:
            route += [(low, high), (high, low)]
    return lax.ppermute(block, axis, route)


def node_width(widths, node_at):
    return jnp.sum(jnp.where(jnp.arange(widths.shape[0]) == node_at, widths, 0))


def chain_fold(flat_chain, tile_width, ancestors, shard_piece):
    piece_rows = shard_piece.shape[1]
    picked = jnp.concatenate(
        [
            lax.dynamic_slice_in_dim(flat_chain, level_at * tile_width, piece_rows, 1)
            for level_at in range(ancestors)
        ],
        axis=1,
    )
    stacked = shard_piece.reshape(ancestors * piece_rows, shard_piece.shape[2])
    return jnp.dot(picked, stacked, preferred_element_type=jnp.float32)


def local_general(
    widths,
    bottom_lists,
    root_inverse,
    second_panels,
    second_inverse,
    third_panels,
    third_inverse,
    bottom_panels,
    bottom_inverse,
):
    group_at = lax.axis_index("leaf")
    row_at = lax.axis_index("row")
    col_at = lax.axis_index("col")
    rows_dev = root_inverse.shape[0]
    tile_width = root_inverse.shape[1]
    half_cols = second_panels.shape[2]
    own_cols = third_panels.shape[3]
    half_at = group_at % 2
    parent_one = 1 + group_at // 2
    node_two = 3 + group_at
    row_first = row_at * rows_dev
    row_index = row_first + jnp.arange(rows_dev)
    root_width = node_width(widths, 0)
    root_mask = (row_index < root_width)[:, None] & (jnp.arange(tile_width) < root_width)[None, :]
    root_block = jnp.where(root_mask, root_inverse, 0)
    width_one = node_width(widths, parent_one)
    mask_rows_one = row_index < width_one
    first_col = half_at * (tile_width // 2) + col_at * half_cols
    mask_cols_one = first_col + jnp.arange(half_cols) < width_one
    panel_one = jnp.where(mask_cols_one[None, :], second_panels[0], 0)
    shard_piece = lax.all_gather(panel_one, "row", axis=0, tiled=True)
    flat_piece = shard_piece
    product_one = jnp.dot(root_block, flat_piece, preferred_element_type=jnp.float32)
    off_one = (-product_one).astype(jnp.bfloat16)
    mine_half = lax.all_gather(off_one, "col", axis=1, tiled=True)
    other_half = partner(mine_half, "leaf", 0)
    off_full = jnp.where(
        half_at == 0,
        jnp.concatenate([mine_half, other_half], 1),
        jnp.concatenate([other_half, mine_half], 1),
    )
    term_one = lax.dot_general(
        panel_one, off_full, (((0,), (0,)), ((), ())), preferred_element_type=jnp.float32
    )
    summed_one = lax.psum_scatter(
        term_one.astype(jnp.bfloat16), "row", scatter_dimension=1, tiled=True
    ).astype(jnp.float32)
    inverse_one = jnp.where(
        mask_cols_one[:, None] & mask_rows_one[None, :], second_inverse[0], 0
    ).astype(jnp.float32)
    diag_one = (inverse_one - summed_one).astype(jnp.bfloat16)
    mine_diag = lax.all_gather(diag_one.T, "col", axis=1, tiled=True)
    other_diag = partner(mine_diag, "leaf", 0)
    diag_full = jnp.where(
        half_at == 0,
        jnp.concatenate([mine_diag, other_diag], 1),
        jnp.concatenate([other_diag, mine_diag], 1),
    )
    second_off = off_one[None]
    second_diag = diag_one[None]
    turned_one = lax.all_to_all(off_full, "row", split_axis=1, concat_axis=0, tiled=True)
    chain_two = jnp.stack(
        [jnp.concatenate([root_block, off_full], 1), jnp.concatenate([turned_one.T, diag_full], 1)],
        0,
    )
    flat_two = chain_two.reshape(2 * rows_dev, 2 * tile_width)
    first_own = col_at * own_cols
    width_two = node_width(widths, node_two)
    mask_cols_two = first_own + jnp.arange(own_cols) < width_two
    panel_two = jnp.where(mask_cols_two[None, None, :], third_panels[0], 0)
    product_two = chain_fold(
        flat_two, tile_width, 2, lax.all_gather(panel_two, "row", axis=1, tiled=True)
    )
    off_two = (-product_two).astype(jnp.bfloat16).reshape(2, rows_dev, own_cols)
    full_two = lax.all_gather(off_two, "col", axis=2, tiled=True)
    term_two = jnp.einsum("kin,kim->nm", panel_two, full_two, preferred_element_type=jnp.float32)
    summed_two = lax.psum_scatter(
        term_two.astype(jnp.bfloat16), "row", scatter_dimension=1, tiled=True
    ).astype(jnp.float32)
    mask_rows_two = row_index < width_two
    inverse_two = jnp.where(
        mask_cols_two[:, None] & mask_rows_two[None, :], third_inverse[0], 0
    ).astype(jnp.float32)
    diag_two = (inverse_two - summed_two).astype(jnp.bfloat16)
    diag_rows_two = lax.all_gather(diag_two.T, "col", axis=1, tiled=True)
    turned_two = lax.all_to_all(full_two, "row", split_axis=2, concat_axis=1, tiled=True)
    lower_two = jnp.transpose(turned_two, (2, 0, 1)).reshape(rows_dev, 2 * tile_width)
    chain_three = jnp.stack(
        [
            jnp.concatenate([chain_two[0], full_two[0]], 1),
            jnp.concatenate([chain_two[1], full_two[1]], 1),
            jnp.concatenate([lower_two, diag_rows_two], 1),
        ],
        0,
    )
    flat_three = chain_three.reshape(3 * rows_dev, 3 * tile_width)
    bottom_dev = bottom_panels.shape[0]
    list_len = bottom_lists.shape[1]
    block_rows = 2 * tile_width // list_len
    node_three = NODES - BOTTOM + bottom_dev * group_at + jnp.arange(bottom_dev)
    width_three = jnp.sum(
        jnp.where(jnp.arange(widths.shape[0])[None, :] == node_three[:, None], widths[None, :], 0),
        1,
    )
    mask_cols_three = (first_own + jnp.arange(own_cols))[None, :] < width_three[:, None]
    panel_three = jnp.where(mask_cols_three[:, None, :], bottom_panels, 0)
    positions = (
        jnp.repeat(bottom_lists, block_rows, axis=1) * block_rows
        + jnp.arange(list_len * block_rows) % block_rows
    )
    own_chain = (jnp.arange(3)[:, None] * tile_width + row_index[None, :]).reshape(-1)
    matches = bottom_lists[:, :, None] == (own_chain // block_rows)[None, None, :]
    member = jnp.any(matches, axis=1)
    slot_index = (
        jnp.sum(jnp.where(matches, jnp.arange(list_len)[None, :, None], 0), axis=1) * block_rows
        + own_chain % block_rows
    )
    shard_piece = lax.all_gather(panel_three, "row", axis=1, tiled=True)
    kept_rows = jnp.zeros((bottom_dev, 3 * rows_dev, own_cols), jnp.bfloat16)
    piece_rows = shard_piece.shape[1]
    columns = jnp.take(flat_three, positions.reshape(-1), axis=1).reshape(
        3 * rows_dev, bottom_dev, piece_rows
    )
    running = jnp.einsum("aec,ecn->ean", columns, shard_piece, preferred_element_type=jnp.float32)
    inside = member & (slot_index >= 0) & (slot_index < piece_rows)
    fetched = jax.vmap(lambda rows_in, picks: jnp.take(rows_in, picks, axis=0))(
        shard_piece, jnp.clip(slot_index, 0, piece_rows - 1)
    )
    kept_rows = jnp.where(inside[:, :, None], fetched, kept_rows)
    product_three, kept_rows = (running, kept_rows)
    chain_rows = kept_rows.reshape(bottom_dev, 3, rows_dev, own_cols)
    off_three = jnp.where(member[:, :, None], -product_three, 0.0).astype(jnp.bfloat16)
    off_three = off_three.reshape(bottom_dev, 3, rows_dev, own_cols)
    full_three = lax.all_gather(off_three, "col", axis=3, tiled=True)
    term_three = jnp.einsum(
        "ekin,ekim->enm", chain_rows, full_three, preferred_element_type=jnp.float32
    )
    summed_three = lax.psum_scatter(
        term_three.astype(jnp.bfloat16), "row", scatter_dimension=2, tiled=True
    ).astype(jnp.float32)
    mask_rows_three = row_index[None, :] < width_three[:, None]
    inverse_three = jnp.where(
        mask_cols_three[:, :, None] & mask_rows_three[:, None, :], bottom_inverse, 0
    ).astype(jnp.float32)
    diag_three = (inverse_three - summed_three).astype(jnp.bfloat16)
    return (second_off, second_diag, off_two[None], diag_two[None], off_three, diag_three)


def copy_block(picks, blocks_in, blocks_out):
    blocks_out[...] = blocks_in[...]


def pick_columns(matrix, picks, width):
    rows = matrix.shape[0]
    count = picks.shape[0]
    return pl.pallas_call(
        copy_block,
        out_shape=jax.ShapeDtypeStruct((rows, count * width), matrix.dtype),
        grid_spec=pltpu.PrefetchScalarGridSpec(
            num_scalar_prefetch=1,
            grid=(count,),
            in_specs=[pl.BlockSpec((rows, width), lambda j, picks: (0, picks[j]))],
            out_specs=pl.BlockSpec((rows, width), lambda j, picks: (0, j)),
        ),
        cost_estimate=pl.CostEstimate(
            flops=0, transcendentals=0, bytes_accessed=4 * rows * count * width
        ),
        name="pick_columns",
    )(picks, matrix)


def pick_rows(matrix, picks, height):
    columns = matrix.shape[1]
    count = picks.shape[0]
    return pl.pallas_call(
        copy_block,
        out_shape=jax.ShapeDtypeStruct((count * height, columns), matrix.dtype),
        grid_spec=pltpu.PrefetchScalarGridSpec(
            num_scalar_prefetch=1,
            grid=(count,),
            in_specs=[pl.BlockSpec((height, columns), lambda j, picks: (picks[j], 0))],
            out_specs=pl.BlockSpec((height, columns), lambda j, picks: (j, 0)),
        ),
        cost_estimate=pl.CostEstimate(
            flops=0, transcendentals=0, bytes_accessed=4 * columns * count * height
        ),
        name="pick_rows",
    )(picks, matrix)


def beside(mine, other, place, axis):
    return jnp.where(
        place == 0,
        jnp.concatenate([mine, other], axis),
        jnp.concatenate([other, mine], axis),
    )


def swap_columns(block):
    return lax.ppermute(block, "col", [(0, 1), (1, 0)])


def both_columns(block, col_at, axis):
    return beside(block, swap_columns(block), col_at, axis)


def row_route(apart):
    return [(at, at ^ apart) for at in range(lax.axis_size("row"))]


def row_exchange(block, row_at):
    count = lax.axis_size("row")
    width = block.shape[1] // count
    own = lax.dynamic_slice_in_dim(block, row_at * width, width, 1)
    turned = jnp.zeros((count,) + own.shape, own.dtype)
    turned = lax.dynamic_update_index_in_dim(turned, own, row_at, 0)
    for apart in range(1, count):
        sent = lax.dynamic_slice_in_dim(block, (row_at ^ apart) * width, width, 1)
        came = lax.ppermute(sent, "row", row_route(apart))
        turned = lax.dynamic_update_index_in_dim(turned, came, row_at ^ apart, 0)
    return turned


def product(left, right):
    return jnp.dot(left, right, preferred_element_type=jnp.float32)


def inner(left, right):
    return lax.dot_general(
        left, right, (((0,), (0,)), ((), ())), preferred_element_type=jnp.float32
    )


def local_paired(
    widths,
    bottom_lists,
    root_inverse,
    second_panels,
    second_inverse,
    third_panels,
    third_inverse,
    bottom_panels,
    bottom_inverse,
):
    group_at = lax.axis_index("leaf")
    row_at = lax.axis_index("row")
    col_at = lax.axis_index("col")
    rows_dev = root_inverse.shape[0]
    tile_width = root_inverse.shape[1]
    half_cols = second_panels.shape[2]
    own_cols = third_panels.shape[3]
    half_at = group_at % 2
    row_first = row_at * rows_dev
    first_own = col_at * own_cols
    row_index = row_first + jnp.arange(rows_dev)
    all_index = jnp.arange(tile_width)
    own_index = first_own + jnp.arange(own_cols)

    root_width = node_width(widths, 0)
    root_mask = (row_index < root_width)[:, None] & (all_index < root_width)[None, :]
    root_block = jnp.where(root_mask, root_inverse, 0)
    count = lax.axis_size("row")
    mine = jnp.zeros((count, rows_dev, half_cols), jnp.bfloat16)
    other = mine
    for apart in range(count):
        came = second_panels[0]
        if apart > 0:
            came = lax.ppermute(came, "row", row_route(apart))
        mine = lax.dynamic_update_index_in_dim(mine, came, row_at ^ apart, 0)
        other = lax.dynamic_update_index_in_dim(other, swap_columns(came), row_at ^ apart, 0)
    panel_half = beside(mine, other, col_at, 2).reshape(tile_width, 2 * half_cols)
    panel_one = beside(panel_half, partner(panel_half, "leaf", 0), half_at, 1)
    inverse_half = both_columns(second_inverse[0], col_at, 0)
    inverse_one = beside(inverse_half, partner(inverse_half, "leaf", 0), half_at, 0)

    width_one = node_width(widths, 1 + group_at // 2)
    keep_one = all_index < width_one
    keep_rows_one = row_index < width_one
    off_one = jnp.where(keep_one[None, :], -product(root_block, panel_one), 0).astype(jnp.bfloat16)
    share_rows = rows_dev // 4
    share_at = 2 * half_at + col_at
    share = lax.dynamic_slice_in_dim(off_one, share_at * share_rows, share_rows, 0)
    turn_share = row_exchange(share, row_at)
    turn_share = both_columns(turn_share, col_at, 1)
    turn_one = beside(turn_share, partner(turn_share, "leaf", 0), half_at, 1)
    turn_one = turn_one.reshape(tile_width, rows_dev)
    mask_one = keep_one[:, None] & keep_rows_one[None, :]
    diag_one = jnp.where(
        mask_one, inverse_one.astype(jnp.float32) - inner(panel_one, turn_one), 0
    ).astype(jnp.bfloat16)
    quarter_first = half_at * (tile_width // 2) + col_at * half_cols
    second_off = lax.dynamic_slice_in_dim(off_one, quarter_first, half_cols, 1)[None]
    second_diag = lax.dynamic_slice_in_dim(diag_one, quarter_first, half_cols, 0)[None]

    panel_two = lax.all_gather(third_panels[0], "row", axis=1, tiled=True)
    panel_root, panel_second = panel_two[0], panel_two[1]
    width_two = node_width(widths, 3 + group_at)
    keep_two = own_index < width_two
    keep_rows_two = row_index < width_two
    mask_two = keep_two[:, None] & keep_rows_two[None, :]
    product_root = product(root_block, panel_root) + product(off_one, panel_second)
    product_second = inner(turn_one, panel_root) + inner(diag_one, panel_second)
    off_two = jnp.stack(
        [
            jnp.where(keep_two[None, :], -part, 0).astype(jnp.bfloat16)
            for part in (product_root, product_second)
        ]
    )
    kept = lax.dynamic_index_in_dim(off_two, col_at, 0, keepdims=False)
    given = lax.dynamic_index_in_dim(off_two, 1 - col_at, 0, keepdims=False)
    share_two = beside(kept, swap_columns(given), col_at, 1)
    turn_mine = row_exchange(share_two, row_at).reshape(tile_width, rows_dev)
    turn_two = both_columns(turn_mine, col_at, 0)
    other_two = beside(given, swap_columns(kept), col_at, 1)
    full_root = jnp.where(col_at == 0, share_two, other_two)
    full_second = jnp.where(col_at == 0, other_two, share_two)
    diag_two = jnp.where(
        mask_two,
        third_inverse[0].astype(jnp.float32)
        - inner(panel_two.reshape(2 * tile_width, own_cols), turn_two),
        0,
    ).astype(jnp.bfloat16)
    diag_full = both_columns(diag_two, col_at, 0)

    bottom_dev = bottom_panels.shape[0]
    list_len = bottom_lists.shape[1]
    block_rows = 2 * tile_width // list_len
    upper_len = list_len - tile_width // block_rows
    upper_rows = upper_len * block_rows
    dev_blocks = rows_dev // block_rows
    upper_blocks = (
        jnp.arange(2)[:, None] * (tile_width // block_rows)
        + row_at * dev_blocks
        + jnp.arange(dev_blocks)[None, :]
    ).reshape(-1)
    from_root = jnp.concatenate([root_block, off_one], 1)
    from_second = jnp.concatenate([turn_one, diag_one], 0)
    uppers = []
    lowers = []
    panels = []
    slots = []
    parent_slots = upper_len + row_at * dev_blocks + jnp.arange(dev_blocks)
    for at in range(bottom_dev):
        listed = bottom_lists[at, :upper_len]
        matches = listed[:, None] == upper_blocks[None, :]
        member_rows = jnp.repeat(jnp.any(matches, axis=0), block_rows)
        upper_slots = jnp.sum(jnp.where(matches, jnp.arange(upper_len)[:, None], 0), axis=0)
        slots.append(jnp.concatenate([upper_slots, parent_slots]).astype(jnp.int32))
        width_three = node_width(widths, NODES - BOTTOM + bottom_dev * group_at + at)
        keep_three = own_index < width_three
        keep_upper = member_rows[:, None] & keep_three[None, :]
        panel = lax.all_gather(bottom_panels[at], "row", axis=0, tiled=True)
        top, low = panel[:upper_rows], panel[upper_rows:]
        listed_root = pick_columns(from_root, listed, block_rows)
        listed_second = pick_rows(from_second, listed, block_rows)
        listed_parent = pick_rows(turn_two, listed, block_rows)
        product_root = product(listed_root, top) + product(full_root, low)
        product_second = inner(listed_second, top) + product(full_second, low)
        upper = jnp.concatenate([product_root, product_second], 0)
        lower = inner(listed_parent, top) + inner(diag_full, low)
        uppers.append(jnp.where(keep_upper, -upper, 0).astype(jnp.bfloat16))
        lowers.append(jnp.where(keep_three[None, :], -lower, 0).astype(jnp.bfloat16))
        panels.append(panel)
    fulls = []
    for at in range(bottom_dev):
        mine = jnp.concatenate([uppers[at], lowers[at]], 0)
        other = jnp.concatenate([swap_columns(uppers[at]), swap_columns(lowers[at])], 0)
        fulls.append(beside(mine, other, col_at, 1))
    diags = []
    for at in range(bottom_dev):
        width_three = node_width(widths, NODES - BOTTOM + bottom_dev * group_at + at)
        mask_three = (own_index < width_three)[:, None] & (row_index < width_three)[None, :]
        term = inner(fulls[at], pick_rows(panels[at], slots[at], block_rows))
        summed = lax.psum_scatter(
            term.astype(jnp.bfloat16), "row", scatter_dimension=0, tiled=True
        ).astype(jnp.float32).T
        diags.append(
            jnp.where(mask_three, bottom_inverse[at].astype(jnp.float32) - summed, 0).astype(
                jnp.bfloat16
            )
        )
    offs = [
        jnp.concatenate([upper, lower], 0).reshape(3, rows_dev, own_cols)
        for upper, lower in zip(uppers, lowers)
    ]
    return (
        second_off,
        second_diag,
        off_two[None],
        diag_two[None],
        jnp.stack(offs),
        jnp.stack(diags),
    )


def solution(mesh):
    in_specs = (
        P(),
        P("leaf", None),
        P("row", None),
        P("leaf", "row", "col"),
        P("leaf", "col", "row"),
        P("leaf", None, "row", "col"),
        P("leaf", "col", "row"),
        P("leaf", "row", "col"),
        P("leaf", "col", "row"),
    )
    out_specs = (
        P("leaf", "row", "col"),
        P("leaf", "col", "row"),
        P("leaf", None, "row", "col"),
        P("leaf", "col", "row"),
        P("leaf", None, "row", "col"),
        P("leaf", "col", "row"),
    )
    if mesh.shape["col"] != 2:
        return jax.shard_map(
            local_general, mesh=mesh, in_specs=in_specs, out_specs=out_specs, check_vma=False
        )

    return jax.shard_map(
        local_paired, mesh=mesh, in_specs=in_specs, out_specs=out_specs, check_vma=False
    )
```

```python
import jax
import jax.numpy as jnp
from jax import lax
from jax.experimental import pallas as pl
from jax.experimental.pallas import tpu as pltpu
from jax.sharding import PartitionSpec as P

NODES = 15
BOTTOM = 8


def partner(block, axis, apart):
    count = lax.axis_size(axis)
    route = []
    for low in range(count):
        high = low | 1 << apart
        if high != low and high < count:
            route += [(low, high), (high, low)]
    return lax.ppermute(block, axis, route)


def node_width(widths, node_at):
    return jnp.sum(jnp.where(jnp.arange(widths.shape[0]) == node_at, widths, 0))


def chain_fold(flat_chain, tile_width, ancestors, shard_piece):
    piece_rows = shard_piece.shape[1]
    picked = jnp.concatenate(
        [
            lax.dynamic_slice_in_dim(flat_chain, level_at * tile_width, piece_rows, 1)
            for level_at in range(ancestors)
        ],
        axis=1,
    )
    stacked = shard_piece.reshape(ancestors * piece_rows, shard_piece.shape[2])
    return jnp.dot(picked, stacked, preferred_element_type=jnp.float32)


def local_general(
    widths,
    bottom_lists,
    root_inverse,
    second_panels,
    second_inverse,
    third_panels,
    third_inverse,
    bottom_panels,
    bottom_inverse,
):
    group_at = lax.axis_index("leaf")
    row_at = lax.axis_index("row")
    col_at = lax.axis_index("col")
    rows_dev = root_inverse.shape[0]
    tile_width = root_inverse.shape[1]
    half_cols = second_panels.shape[2]
    own_cols = third_panels.shape[3]
    half_at = group_at % 2
    parent_one = 1 + group_at // 2
    node_two = 3 + group_at
    row_first = row_at * rows_dev
    row_index = row_first + jnp.arange(rows_dev)
    root_width = node_width(widths, 0)
    root_mask = (row_index < root_width)[:, None] & (jnp.arange(tile_width) < root_width)[None, :]
    root_block = jnp.where(root_mask, root_inverse, 0)
    width_one = node_width(widths, parent_one)
    mask_rows_one = row_index < width_one
    first_col = half_at * (tile_width // 2) + col_at * half_cols
    mask_cols_one = first_col + jnp.arange(half_cols) < width_one
    panel_one = jnp.where(mask_cols_one[None, :], second_panels[0], 0)
    shard_piece = lax.all_gather(panel_one, "row", axis=0, tiled=True)
    flat_piece = shard_piece
    product_one = jnp.dot(root_block, flat_piece, preferred_element_type=jnp.float32)
    off_one = (-product_one).astype(jnp.bfloat16)
    mine_half = lax.all_gather(off_one, "col", axis=1, tiled=True)
    other_half = partner(mine_half, "leaf", 0)
    off_full = jnp.where(
        half_at == 0,
        jnp.concatenate([mine_half, other_half], 1),
        jnp.concatenate([other_half, mine_half], 1),
    )
    term_one = lax.dot_general(
        panel_one, off_full, (((0,), (0,)), ((), ())), preferred_element_type=jnp.float32
    )
    summed_one = lax.psum_scatter(
        term_one.astype(jnp.bfloat16), "row", scatter_dimension=1, tiled=True
    ).astype(jnp.float32)
    inverse_one = jnp.where(
        mask_cols_one[:, None] & mask_rows_one[None, :], second_inverse[0], 0
    ).astype(jnp.float32)
    diag_one = (inverse_one - summed_one).astype(jnp.bfloat16)
    mine_diag = lax.all_gather(diag_one.T, "col", axis=1, tiled=True)
    other_diag = partner(mine_diag, "leaf", 0)
    diag_full = jnp.where(
        half_at == 0,
        jnp.concatenate([mine_diag, other_diag], 1),
        jnp.concatenate([other_diag, mine_diag], 1),
    )
    second_off = off_one[None]
    second_diag = diag_one[None]
    turned_one = lax.all_to_all(off_full, "row", split_axis=1, concat_axis=0, tiled=True)
    chain_two = jnp.stack(
        [jnp.concatenate([root_block, off_full], 1), jnp.concatenate([turned_one.T, diag_full], 1)],
        0,
    )
    flat_two = chain_two.reshape(2 * rows_dev, 2 * tile_width)
    first_own = col_at * own_cols
    width_two = node_width(widths, node_two)
    mask_cols_two = first_own + jnp.arange(own_cols) < width_two
    panel_two = jnp.where(mask_cols_two[None, None, :], third_panels[0], 0)
    product_two = chain_fold(
        flat_two, tile_width, 2, lax.all_gather(panel_two, "row", axis=1, tiled=True)
    )
    off_two = (-product_two).astype(jnp.bfloat16).reshape(2, rows_dev, own_cols)
    full_two = lax.all_gather(off_two, "col", axis=2, tiled=True)
    term_two = jnp.einsum("kin,kim->nm", panel_two, full_two, preferred_element_type=jnp.float32)
    summed_two = lax.psum_scatter(
        term_two.astype(jnp.bfloat16), "row", scatter_dimension=1, tiled=True
    ).astype(jnp.float32)
    mask_rows_two = row_index < width_two
    inverse_two = jnp.where(
        mask_cols_two[:, None] & mask_rows_two[None, :], third_inverse[0], 0
    ).astype(jnp.float32)
    diag_two = (inverse_two - summed_two).astype(jnp.bfloat16)
    diag_rows_two = lax.all_gather(diag_two.T, "col", axis=1, tiled=True)
    turned_two = lax.all_to_all(full_two, "row", split_axis=2, concat_axis=1, tiled=True)
    lower_two = jnp.transpose(turned_two, (2, 0, 1)).reshape(rows_dev, 2 * tile_width)
    chain_three = jnp.stack(
        [
            jnp.concatenate([chain_two[0], full_two[0]], 1),
            jnp.concatenate([chain_two[1], full_two[1]], 1),
            jnp.concatenate([lower_two, diag_rows_two], 1),
        ],
        0,
    )
    flat_three = chain_three.reshape(3 * rows_dev, 3 * tile_width)
    bottom_dev = bottom_panels.shape[0]
    list_len = bottom_lists.shape[1]
    block_rows = 2 * tile_width // list_len
    node_three = NODES - BOTTOM + bottom_dev * group_at + jnp.arange(bottom_dev)
    width_three = jnp.sum(
        jnp.where(jnp.arange(widths.shape[0])[None, :] == node_three[:, None], widths[None, :], 0),
        1,
    )
    mask_cols_three = (first_own + jnp.arange(own_cols))[None, :] < width_three[:, None]
    panel_three = jnp.where(mask_cols_three[:, None, :], bottom_panels, 0)
    positions = (
        jnp.repeat(bottom_lists, block_rows, axis=1) * block_rows
        + jnp.arange(list_len * block_rows) % block_rows
    )
    own_chain = (jnp.arange(3)[:, None] * tile_width + row_index[None, :]).reshape(-1)
    matches = bottom_lists[:, :, None] == (own_chain // block_rows)[None, None, :]
    member = jnp.any(matches, axis=1)
    slot_index = (
        jnp.sum(jnp.where(matches, jnp.arange(list_len)[None, :, None], 0), axis=1) * block_rows
        + own_chain % block_rows
    )
    shard_piece = lax.all_gather(panel_three, "row", axis=1, tiled=True)
    kept_rows = jnp.zeros((bottom_dev, 3 * rows_dev, own_cols), jnp.bfloat16)
    piece_rows = shard_piece.shape[1]
    columns = jnp.take(flat_three, positions.reshape(-1), axis=1).reshape(
        3 * rows_dev, bottom_dev, piece_rows
    )
    running = jnp.einsum("aec,ecn->ean", columns, shard_piece, preferred_element_type=jnp.float32)
    inside = member & (slot_index >= 0) & (slot_index < piece_rows)
    fetched = jax.vmap(lambda rows_in, picks: jnp.take(rows_in, picks, axis=0))(
        shard_piece, jnp.clip(slot_index, 0, piece_rows - 1)
    )
    kept_rows = jnp.where(inside[:, :, None], fetched, kept_rows)
    product_three, kept_rows = (running, kept_rows)
    chain_rows = kept_rows.reshape(bottom_dev, 3, rows_dev, own_cols)
    off_three = jnp.where(member[:, :, None], -product_three, 0.0).astype(jnp.bfloat16)
    off_three = off_three.reshape(bottom_dev, 3, rows_dev, own_cols)
    full_three = lax.all_gather(off_three, "col", axis=3, tiled=True)
    term_three = jnp.einsum(
        "ekin,ekim->enm", chain_rows, full_three, preferred_element_type=jnp.float32
    )
    summed_three = lax.psum_scatter(
        term_three.astype(jnp.bfloat16), "row", scatter_dimension=2, tiled=True
    ).astype(jnp.float32)
    mask_rows_three = row_index[None, :] < width_three[:, None]
    inverse_three = jnp.where(
        mask_cols_three[:, :, None] & mask_rows_three[:, None, :], bottom_inverse, 0
    ).astype(jnp.float32)
    diag_three = (inverse_three - summed_three).astype(jnp.bfloat16)
    return (second_off, second_diag, off_two[None], diag_two[None], off_three, diag_three)


def copy_block(picks, blocks_in, blocks_out):
    blocks_out[...] = blocks_in[...]


def pick_columns(matrix, picks, width):
    rows = matrix.shape[0]
    count = picks.shape[0]
    return pl.pallas_call(
        copy_block,
        out_shape=jax.ShapeDtypeStruct((rows, count * width), matrix.dtype),
        grid_spec=pltpu.PrefetchScalarGridSpec(
            num_scalar_prefetch=1,
            grid=(count,),
            in_specs=[pl.BlockSpec((rows, width), lambda j, picks: (0, picks[j]))],
            out_specs=pl.BlockSpec((rows, width), lambda j, picks: (0, j)),
        ),
        cost_estimate=pl.CostEstimate(
            flops=0, transcendentals=0, bytes_accessed=4 * rows * count * width
        ),
        name="pick_columns",
    )(picks, matrix)


def pick_rows(matrix, picks, height):
    columns = matrix.shape[1]
    count = picks.shape[0]
    return pl.pallas_call(
        copy_block,
        out_shape=jax.ShapeDtypeStruct((count * height, columns), matrix.dtype),
        grid_spec=pltpu.PrefetchScalarGridSpec(
            num_scalar_prefetch=1,
            grid=(count,),
            in_specs=[pl.BlockSpec((height, columns), lambda j, picks: (picks[j], 0))],
            out_specs=pl.BlockSpec((height, columns), lambda j, picks: (j, 0)),
        ),
        cost_estimate=pl.CostEstimate(
            flops=0, transcendentals=0, bytes_accessed=4 * columns * count * height
        ),
        name="pick_rows",
    )(picks, matrix)


def beside(mine, other, place, axis):
    return jnp.where(
        place == 0,
        jnp.concatenate([mine, other], axis),
        jnp.concatenate([other, mine], axis),
    )


def swap_columns(block):
    return lax.ppermute(block, "col", [(0, 1), (1, 0)])


def both_columns(block, col_at, axis):
    return beside(block, swap_columns(block), col_at, axis)


def row_route(apart):
    return [(at, at ^ apart) for at in range(lax.axis_size("row"))]


def row_exchange(block, row_at):
    count = lax.axis_size("row")
    width = block.shape[1] // count
    own = lax.dynamic_slice_in_dim(block, row_at * width, width, 1)
    turned = jnp.zeros((count,) + own.shape, own.dtype)
    turned = lax.dynamic_update_index_in_dim(turned, own, row_at, 0)
    for apart in range(1, count):
        sent = lax.dynamic_slice_in_dim(block, (row_at ^ apart) * width, width, 1)
        came = lax.ppermute(sent, "row", row_route(apart))
        turned = lax.dynamic_update_index_in_dim(turned, came, row_at ^ apart, 0)
    return turned


def product(left, right):
    return jnp.dot(left, right, preferred_element_type=jnp.float32)


def inner(left, right):
    return lax.dot_general(
        left, right, (((0,), (0,)), ((), ())), preferred_element_type=jnp.float32
    )


def local_paired(
    widths,
    bottom_lists,
    root_inverse,
    second_panels,
    second_inverse,
    third_panels,
    third_inverse,
    bottom_panels,
    bottom_inverse,
):
    group_at = lax.axis_index("leaf")
    row_at = lax.axis_index("row")
    col_at = lax.axis_index("col")
    rows_dev = root_inverse.shape[0]
    tile_width = root_inverse.shape[1]
    half_cols = second_panels.shape[2]
    own_cols = third_panels.shape[3]
    half_at = group_at % 2
    row_first = row_at * rows_dev
    first_own = col_at * own_cols
    row_index = row_first + jnp.arange(rows_dev)
    all_index = jnp.arange(tile_width)
    own_index = first_own + jnp.arange(own_cols)

    root_width = node_width(widths, 0)
    root_mask = (row_index < root_width)[:, None] & (all_index < root_width)[None, :]
    root_block = jnp.where(root_mask, root_inverse, 0)
    count = lax.axis_size("row")
    mine = jnp.zeros((count, rows_dev, half_cols), jnp.bfloat16)
    other = mine
    for apart in range(count):
        came = second_panels[0]
        if apart > 0:
            came = lax.ppermute(came, "row", row_route(apart))
        mine = lax.dynamic_update_index_in_dim(mine, came, row_at ^ apart, 0)
        other = lax.dynamic_update_index_in_dim(other, swap_columns(came), row_at ^ apart, 0)
    panel_half = beside(mine, other, col_at, 2).reshape(tile_width, 2 * half_cols)
    panel_one = beside(panel_half, partner(panel_half, "leaf", 0), half_at, 1)
    inverse_half = both_columns(second_inverse[0], col_at, 0)
    inverse_one = beside(inverse_half, partner(inverse_half, "leaf", 0), half_at, 0)

    width_one = node_width(widths, 1 + group_at // 2)
    keep_one = all_index < width_one
    keep_rows_one = row_index < width_one
    off_one = jnp.where(keep_one[None, :], -product(root_block, panel_one), 0).astype(jnp.bfloat16)
    share_rows = rows_dev // 4
    share_at = 2 * half_at + col_at
    share = lax.dynamic_slice_in_dim(off_one, share_at * share_rows, share_rows, 0)
    turn_share = row_exchange(share, row_at)
    turn_share = both_columns(turn_share, col_at, 1)
    turn_one = beside(turn_share, partner(turn_share, "leaf", 0), half_at, 1)
    turn_one = turn_one.reshape(tile_width, rows_dev)
    mask_one = keep_one[:, None] & keep_rows_one[None, :]
    diag_one = jnp.where(
        mask_one, inverse_one.astype(jnp.float32) - inner(panel_one, turn_one), 0
    ).astype(jnp.bfloat16)
    quarter_first = half_at * (tile_width // 2) + col_at * half_cols
    second_off = lax.dynamic_slice_in_dim(off_one, quarter_first, half_cols, 1)[None]
    second_diag = lax.dynamic_slice_in_dim(diag_one, quarter_first, half_cols, 0)[None]

    panel_two = lax.all_gather(third_panels[0], "row", axis=1, tiled=True)
    panel_root, panel_second = panel_two[0], panel_two[1]
    width_two = node_width(widths, 3 + group_at)
    keep_two = own_index < width_two
    keep_rows_two = row_index < width_two
    mask_two = keep_two[:, None] & keep_rows_two[None, :]
    product_root = product(root_block, panel_root) + product(off_one, panel_second)
    product_second = inner(turn_one, panel_root) + inner(diag_one, panel_second)
    off_two = jnp.stack(
        [
            jnp.where(keep_two[None, :], -part, 0).astype(jnp.bfloat16)
            for part in (product_root, product_second)
        ]
    )
    kept = lax.dynamic_index_in_dim(off_two, col_at, 0, keepdims=False)
    given = lax.dynamic_index_in_dim(off_two, 1 - col_at, 0, keepdims=False)
    share_two = beside(kept, swap_columns(given), col_at, 1)
    turn_mine = row_exchange(share_two, row_at).reshape(tile_width, rows_dev)
    turn_two = both_columns(turn_mine, col_at, 0)
    other_two = beside(given, swap_columns(kept), col_at, 1)
    full_root = jnp.where(col_at == 0, share_two, other_two)
    full_second = jnp.where(col_at == 0, other_two, share_two)
    diag_two = jnp.where(
        mask_two,
        third_inverse[0].astype(jnp.float32)
        - inner(panel_two.reshape(2 * tile_width, own_cols), turn_two),
        0,
    ).astype(jnp.bfloat16)
    diag_full = both_columns(diag_two, col_at, 0)

    bottom_dev = bottom_panels.shape[0]
    list_len = bottom_lists.shape[1]
    block_rows = 2 * tile_width // list_len
    upper_len = list_len - tile_width // block_rows
    upper_rows = upper_len * block_rows
    dev_blocks = rows_dev // block_rows
    upper_blocks = (
        jnp.arange(2)[:, None] * (tile_width // block_rows)
        + row_at * dev_blocks
        + jnp.arange(dev_blocks)[None, :]
    ).reshape(-1)
    from_root = jnp.concatenate([root_block, off_one], 1)
    from_second = jnp.concatenate([turn_one, diag_one], 0)
    offs = []
    diags = []
    parent_slots = upper_len + row_at * dev_blocks + jnp.arange(dev_blocks)
    for at in range(bottom_dev):
        last = at + 1 == bottom_dev
        listed = bottom_lists[at, :upper_len]
        matches = listed[:, None] == upper_blocks[None, :]
        member_rows = jnp.repeat(jnp.any(matches, axis=0), block_rows)
        upper_slots = jnp.sum(jnp.where(matches, jnp.arange(upper_len)[:, None], 0), axis=0)
        slots = jnp.concatenate([upper_slots, parent_slots]).astype(jnp.int32)
        width_three = node_width(widths, NODES - BOTTOM + bottom_dev * group_at + at)
        keep_three = own_index < width_three
        listed_root = pick_columns(from_root, listed, block_rows)
        listed_second = pick_rows(from_second, listed, block_rows)
        listed_parent = pick_rows(turn_two, listed, block_rows)
        edges = [0, own_cols * 3 // 4, own_cols] if last else [0, own_cols]
        mine = []
        other = []
        kept = []
        for low_edge, high_edge in zip(edges, edges[1:]):
            keep_piece = keep_three[low_edge:high_edge][None, :]
            panel = lax.all_gather(
                bottom_panels[at, :, low_edge:high_edge], "row", axis=0, tiled=True
            )
            top, low = panel[:upper_rows], panel[upper_rows:]
            product_root = product(listed_root, top) + product(full_root, low)
            product_second = inner(listed_second, top) + product(full_second, low)
            upper = jnp.concatenate([product_root, product_second], 0)
            lower = inner(listed_parent, top) + inner(diag_full, low)
            upper = jnp.where(member_rows[:, None] & keep_piece, -upper, 0).astype(jnp.bfloat16)
            lower = jnp.where(keep_piece, -lower, 0).astype(jnp.bfloat16)
            other_upper = swap_columns(upper)
            other_lower = swap_columns(lower)
            mine.append(jnp.concatenate([upper, lower], 0))
            other.append(jnp.concatenate([other_upper, other_lower], 0))
            kept.append(pick_rows(panel, slots, block_rows))
        offs.append(jnp.concatenate(mine, 1).reshape(3, rows_dev, own_cols))
        kept = lax.optimization_barrier(jnp.concatenate(kept, 1))
        terms = [
            jnp.concatenate([inner(part, kept).astype(jnp.bfloat16) for part in parts], 0)
            for parts in (mine, other)
        ]
        term = beside(*terms, col_at, 0)
        summed = lax.psum_scatter(term, "row", scatter_dimension=0, tiled=True)
        mask_three = keep_three[:, None] & (row_index < width_three)[None, :]
        diags.append(
            jnp.where(
                mask_three,
                bottom_inverse[at].astype(jnp.float32) - summed.astype(jnp.float32).T,
                0,
            ).astype(jnp.bfloat16)
        )
    return (
        second_off,
        second_diag,
        off_two[None],
        diag_two[None],
        jnp.stack(offs),
        jnp.stack(diags),
    )


def solution(mesh):
    in_specs = (
        P(),
        P("leaf", None),
        P("row", None),
        P("leaf", "row", "col"),
        P("leaf", "col", "row"),
        P("leaf", None, "row", "col"),
        P("leaf", "col", "row"),
        P("leaf", "row", "col"),
        P("leaf", "col", "row"),
    )
    out_specs = (
        P("leaf", "row", "col"),
        P("leaf", "col", "row"),
        P("leaf", None, "row", "col"),
        P("leaf", "col", "row"),
        P("leaf", None, "row", "col"),
        P("leaf", "col", "row"),
    )
    if mesh.shape["col"] != 2:
        return jax.shard_map(
            local_general, mesh=mesh, in_specs=in_specs, out_specs=out_specs, check_vma=False
        )

    return jax.shard_map(
        local_paired, mesh=mesh, in_specs=in_specs, out_specs=out_specs, check_vma=False
    )
```
